256 devices in a mesh: dir: 8 (over z), row: 32 (over x, y, core).
Axes of the slice: x: 4, y: 4, z: 8, core: 2. Of those that a mesh axis runs over, the one named last changes fastest.
Arguments:
- influence: bfloat16 [3, 128, 192, 144], P(None, 'row'), may hold values from -0.5 to 0.5
- foot_rows: int32 [8, 3, 128], P('dir', None, 'row'), may hold values from 0 to 127, as said below
- foot_columns: int32 [8, 3, 160], P('dir'), may hold values from 0 to 191
- actuator_codes: int32 [3, 48, 48], replicated, may hold values from 0 to 8191, as said below
- poke_rows: int32 [2048], replicated, may hold values from 0 to 8191, as said below
- subaperture_valid: int32 [8, 64, 80], P('dir', 'row'), may hold values 0 or 1
Outputs:
- interaction: bfloat16 [6912, 8, 10240], P(('dir', 'row'))
The draws below stay inside these ranges and needn't reach their ends.
Inputs may be any that keep to these rules, and one draw needn't show every extreme that they name: `foot_rows`: for every direction, mirror and pupil row y the surface row lies within 2 rows of y, and in every draw some lie exactly 2 rows above and some exactly 2 rows below their pupil row. `actuator_codes`: all entries are distinct. `poke_rows`: all entries are distinct.
All inputs are finite; a program needn't handle non-finite values. No bound on the sum of `subaperture_valid` on one device may be relied on, other than what follows from the above.
Results may differ from the reference program's by a relative error of at most 0.01.
Values may be sent and summed in bfloat16 or wider, within the bound.
A program may use at most 64 MiB of HBM per device.

```python
import jax
import jax.numpy as jnp
from jax import lax

NDM = 3
NAR = 48
NA = 48
BAND = 3
NSUBC = 80
NSC = 192
REACH = 2
NCODE = 8192
POKES = 2048
ACTS = 6912
NAS = 144
NPC = 160
NSUB = 64
NSR = 128
NDIR = 8


def draw_foot_rows(key, part):
    offsets = jax.random.randint(jax.random.fold_in(key, 11), (NDIR, NDM, 1), -REACH, REACH + 1)
    offsets = offsets.at[0, 0, 0].set(REACH).at[0, 1, 0].set(-REACH)
    jitter = jax.random.randint(jax.random.fold_in(key, 12), (NDIR, NDM, NSR), -1, 2)
    pupil_rows = jnp.arange(NSR, dtype=jnp.int32)[None, None, :]
    target = jnp.clip(pupil_rows + offsets + jitter, pupil_rows - REACH, pupil_rows + REACH)
    return jnp.clip(target, 0, NSR - 1).astype(jnp.int32)


def draw_foot_columns(key, part):
    margin = (NSC - NPC) // 2
    offsets = jax.random.randint(jax.random.fold_in(key, 21), (NDIR, NDM, 1), -margin, margin + 1)
    jitter = jax.random.randint(jax.random.fold_in(key, 22), (NDIR, NDM, NPC), -1, 2)
    pupil_columns = jnp.arange(NPC, dtype=jnp.int32)[None, None, :]
    return jnp.clip(pupil_columns + margin + offsets + jitter, 0, NSC - 1).astype(jnp.int32)


def draw_actuator_codes(key, part):
    shuffled = jax.random.permutation(jax.random.fold_in(key, 31), NCODE)
    return shuffled[:ACTS].reshape(NDM, NAR, NA).astype(jnp.int32)


def draw_poke_rows(key, part):
    shuffled = jax.random.permutation(jax.random.fold_in(key, 41), NCODE)
    return shuffled[:POKES].astype(jnp.int32)


def plant(array, key, smallest, high):
    index_at = [jax.random.randint(jax.random.fold_in(key, axis), (), 0, length) for axis, length in enumerate(array.shape)]
    widest = array.shape.index(max(array.shape))
    beside = index_at[:widest] + [(index_at[widest] + 1) % array.shape[widest]] + index_at[widest + 1:]
    return array.at[tuple(index_at)].set(smallest).at[tuple(beside)].set(high)


def steps_of(own_key, extent, pieces, low, high):
    def one(position, blocks):
        steps = jax.random.uniform(jax.random.fold_in(jax.random.fold_in(own_key, 6), position), (blocks,), jnp.float32, low / len(pieces), high / len(pieces))
        return jnp.repeat(jnp.exp(steps), extent[position] // blocks).reshape((-1,) + (1,) * (len(extent) - position - 1))

    level = one(*pieces[0])
    for cut in pieces[1:]:
        level = level * one(*cut)
    return level


def noise(stream_key, extent, deviation, reach, cuts=(), kind=jnp.bfloat16):
    factor_of = steps_of(stream_key, extent, cuts, -0.22, 0.18) if cuts else 1.0
    array = jax.random.normal(stream_key, extent, jnp.float32) * deviation * factor_of
    return jnp.minimum(jnp.maximum(array, -reach), reach).astype(kind)


def setup_inputs(seed: int = 0) -> dict:
    streams_of = jax.random.split(jax.random.key(seed), 7)
    influence = noise(streams_of[0], (NDM, NSR, NSC, NAS), NAS ** -0.5, 0.5, ((1, 32),))
    foot_rows = draw_foot_rows(jax.random.fold_in(streams_of[6], 71), 0)
    foot_columns = draw_foot_columns(jax.random.fold_in(streams_of[6], 71), 0)
    actuator_codes = draw_actuator_codes(jax.random.fold_in(streams_of[6], 71), 0)
    poke_rows = draw_poke_rows(jax.random.fold_in(streams_of[6], 71), 0)
    subaperture_valid = plant((jax.random.randint(streams_of[5], (NDIR, NSUB, NSUBC), 0, 5) < 4).astype(jnp.int32), jax.random.fold_in(streams_of[5], 1), 0, 1)
    return {"influence": influence, "foot_rows": foot_rows, "foot_columns": foot_columns, "actuator_codes": actuator_codes, "poke_rows": poke_rows, "subaperture_valid": subaperture_valid}


def parity_sign(code_values, row_values):
    folded = jnp.bitwise_and(code_values, row_values)
    for stride in (16, 8, 4, 2, 1):
        folded = jnp.bitwise_xor(folded, jnp.right_shift(folded, stride))
    return (1 - 2 * jnp.bitwise_and(folded, 1)).astype(jnp.float32)


def direction_slopes(influence, rows_one, columns_one, valid_one, actuator_codes, poke_rows):
    pupil_phase = jnp.zeros((NSR, NPC, POKES), jnp.float32)
    slot_index = jnp.arange(BAND * NA, dtype=jnp.int32)
    for mirror in range(NDM):
        sampled = influence[mirror][rows_one[mirror]][:, columns_one[mirror]].astype(jnp.float32)
        band_start = jnp.clip(rows_one[mirror] * NAR // NSR - 1, 0, NAR - BAND).astype(jnp.int32)
        code_index = band_start[:, None] * NA + slot_index[None, :]
        column_code = actuator_codes[mirror].reshape(-1)[code_index]
        commands = parity_sign(column_code[:, :, None], poke_rows[None, None, :])
        surface = jnp.einsum("yxa,yap->yxp", sampled, commands, precision=lax.Precision.HIGHEST).astype(jnp.bfloat16)
        pupil_phase = pupil_phase + surface.astype(jnp.float32)
    blocks = pupil_phase.reshape(NSUB, 2, NSUBC, 2, POKES)
    slope_across = 0.5 * ((blocks[:, 0, :, 1] - blocks[:, 0, :, 0]) + (blocks[:, 1, :, 1] - blocks[:, 1, :, 0]))
    slope_down = 0.5 * ((blocks[:, 1, :, 0] - blocks[:, 0, :, 0]) + (blocks[:, 1, :, 1] - blocks[:, 0, :, 1]))
    valid_mask = valid_one.astype(jnp.float32)[:, None, :, None]
    slopes = (jnp.stack([slope_across, slope_down], axis=1) * valid_mask).astype(jnp.bfloat16)
    return slopes.reshape(NSUB * 2 * NSUBC, POKES)


def reference(influence, foot_rows, foot_columns, actuator_codes, poke_rows, subaperture_valid):
    sign_table = parity_sign(actuator_codes.reshape(-1)[:, None], poke_rows[None, :])
    norm_factor = POKES ** -0.5

    def one_direction(direction):
        slopes = direction_slopes(influence, foot_rows[direction], foot_columns[direction],
                                  subaperture_valid[direction], actuator_codes, poke_rows)
        decoded = jnp.dot(sign_table, slopes.astype(jnp.float32).T, precision=lax.Precision.HIGHEST)
        return (decoded * norm_factor).astype(jnp.bfloat16)

    per_direction = lax.map(one_direction, jnp.arange(NDIR, dtype=jnp.int32))
    return jnp.transpose(per_direction, (1, 0, 2))
```

```python
import functools

import jax
import jax.numpy as jnp
from jax import lax
from jax.experimental import pallas as pl
from jax.experimental.pallas import tpu as pltpu
from jax.sharding import PartitionSpec as P

NAR = 48
NA = 48
BAND = 3
REACH = 2
SPAN = 7
MESH = pl.DeviceIdType.MESH
ANY = pl.BlockSpec(memory_space=pl.ANY)
VMEM = pl.BlockSpec(memory_space=pltpu.VMEM)
SMEM = pl.BlockSpec(memory_space=pltpu.SMEM)


def sign_of(code_values, row_values):
    odd = jnp.bitwise_and(lax.population_count(jnp.bitwise_and(code_values, row_values)), 1)
    return jnp.where(odd == 0, 1.0, -1.0).astype(jnp.bfloat16)


def gram_kernel(n_dir, n_row, mine, pokes_lane, pokes_col, local, own, feet, cols,
                gram, partner, above, below, all_feet, all_cols,
                left, right, halo_send, halo_recv, pair_send, pair_recv,
                feet_send, feet_recv, cols_send, cols_recv):
    me_dir, me = lax.axis_index("dir"), lax.axis_index("row")
    core = lax.rem(me, 2)
    chip = me - core

    def row_of(step):
        return lax.rem(me + step + n_row, n_row)

    def other_core():
        return chip + 1 - core

    barrier = pltpu.get_barrier_semaphore()
    up_from = lax.rem(chip - 1 + n_row, n_row)
    down_from = lax.rem(chip + 2, n_row)
    for source in (up_from, down_from):
        pl.semaphore_signal(barrier, inc=1, device_id=(me_dir, source), device_id_type=MESH)
    for hop in range(n_dir):
        there = lax.rem(me_dir + hop, n_dir)
        if hop:
            pl.semaphore_signal(barrier, inc=1, device_id=(there, me), device_id_type=MESH)
        pl.semaphore_signal(barrier, inc=1, device_id=(there, other_core()), device_id_type=MESH)
    pl.semaphore_wait(barrier, 2 * n_dir + 1)

    copies = []

    def send(src, dst, send_sem, recv_sem, target):
        copy = pltpu.make_async_remote_copy(
            src_ref=src, dst_ref=dst, send_sem=send_sem, recv_sem=recv_sem,
            device_id=target, device_id_type=MESH,
        )
        copy.start()
        copies.append(copy)

    rows = own.shape[1]
    next_chip = lax.rem(chip + 2, n_row)
    prev_chip = lax.rem(chip - 2 + n_row, n_row)

    def halo(k, slot, to_core):
        edge = own.at[:, pl.ds(rows - REACH, REACH)] if k == 0 else own.at[:, pl.ds(0, REACH)]
        landing = above if k == 0 else below
        target = (next_chip if k == 0 else prev_chip) + to_core
        return pltpu.make_async_remote_copy(
            src_ref=edge, dst_ref=landing, send_sem=halo_send.at[to_core], recv_sem=halo_recv.at[k],
            device_id=(me_dir, target), device_id_type=MESH,
        )

    @pl.when(core == 1)
    def _():
        for to_core in range(2):
            halo(0, 0, to_core).start()

    @pl.when(core == 0)
    def _():
        for to_core in range(2):
            halo(1, 0, to_core).start()

    send(own, partner, pair_send, pair_recv, (me_dir, other_core()))
    for hop in range(n_dir):
        there = lax.rem(me_dir + hop, n_dir)
        if hop:
            send(feet, all_feet.at[core, me_dir], feet_send.at[hop, 0], feet_recv.at[hop, 0], (there, me))
            send(cols, all_cols.at[me_dir], cols_send.at[hop], cols_recv.at[hop], (there, me))
        send(feet, all_feet.at[core, me_dir], feet_send.at[hop, 1], feet_recv.at[hop, 1],
             (there, other_core()))
    local_feet = pltpu.make_async_copy(feet, all_feet.at[core, me_dir], feet_send.at[0, 0])
    local_feet.start()
    local_cols = pltpu.make_async_copy(cols, all_cols.at[me_dir], cols_send.at[0])
    local_cols.start()

    n_mine, n_poke = left.shape
    tile = 48

    @pl.loop(0, n_mine // tile)
    def _(step):
        at = pl.ds(pl.multiple_of(step * tile, tile), tile)
        left[at, :] = sign_of(mine[at, :], pokes_lane[...])

    high = 128

    @pl.loop(0, n_poke // high)
    def _(step):
        at = pl.ds(pl.multiple_of(step * high, high), high)
        right[at, :] = sign_of(local[...], pokes_col[at, :])

    gram[...] = jnp.dot(left[...], right[...], preferred_element_type=jnp.float32).astype(gram.dtype)

    local_feet.wait()
    local_cols.wait()
    for copy in copies:
        copy.wait()

    @pl.when(core == 1)
    def _():
        for to_core in range(2):
            halo(0, 0, to_core).wait_send()

    @pl.when(core == 0)
    def _():
        for to_core in range(2):
            halo(1, 0, to_core).wait_send()

    halo(0, 0, 0).wait_recv()
    halo(1, 0, 0).wait_recv()


def apply_kernel(feet, place, gram, own, partner, above, below, cols, mask, out,
                 window, sums, weights, staged, sems):
    core = lax.rem(lax.axis_index("row"), 2)
    rows = own.shape[1]
    loads = [
        pltpu.make_async_copy(above, window.at[:, pl.ds(0, REACH)], sems.at[0]),
        pltpu.make_async_copy(own, window.at[:, pl.ds(REACH + rows * core, rows)], sems.at[1]),
        pltpu.make_async_copy(partner, window.at[:, pl.ds(REACH + rows * (1 - core), rows)], sems.at[2]),
        pltpu.make_async_copy(below, window.at[:, pl.ds(REACH + 2 * rows, REACH)], sems.at[3]),
    ]
    for load in loads:
        load.start()
    for load in loads:
        load.wait()
    mirrors, window_rows, slots, columns = window.shape
    n_dir = mask.shape[0]
    wide = cols.shape[-1]
    lane = lax.broadcasted_iota(jnp.int32, (1, wide), 1)
    col_id = lax.broadcasted_iota(jnp.int32, (columns, wide), 0)

    @pl.loop(0, n_dir)
    def _(d):
        sums[...] = jnp.zeros_like(sums)
        for k in range(mirrors):
            for i in range(rows):
                later = cols[d, 8 * k + i, :][None, :]
                first = cols[d, 8 * k + 4 + i, :][None, :]
                turn = jnp.where(lane < 32 * i + 80, -1.0, 1.0)
                odd = jnp.where(col_id == later, 1.0, 0.0) + jnp.where(col_id == first, turn, 0.0)
                even = odd * (-turn)
                for a in range(2):
                    y = 2 * i + a
                    w = feet[y // rows, d, 0, 384 + rows * k + y % rows]
                    part = jnp.dot(
                        window[k, w], (odd if a else even).astype(jnp.bfloat16),
                        preferred_element_type=jnp.float32,
                    )
                    at = pl.ds(pl.multiple_of(place[w] + k * SPAN * NA, NA), slots)
                    sums[at, pl.ds(128 * i, wide)] += part
        weights[...] = sums[...].astype(jnp.bfloat16)
        part = jnp.dot(gram[...], weights[...], preferred_element_type=jnp.float32)
        part = part * mask[d, :][None, :]
        n = staged.shape[1] // n_dir
        for t in range(staged.shape[0]):
            staged[t, pl.ds(d, n, stride=n_dir), :] = part[:, 128 * t : 128 * (t + 1)]

    step = 27

    @pl.loop(0, out.shape[0] // step)
    def _(b):
        for t in range(staged.shape[0]):
            block = staged[t, pl.ds(pl.multiple_of(b * step * n_dir, n_dir), step * n_dir), :]
            block = block.reshape(step, n_dir, 128).astype(out.dtype)
            out[pl.ds(b * step, step), :, 128 * t : 128 * (t + 1)] = block


AROUND = (
    (0, 1), (1, 0), (0, 3), (3, 0), (1, 1), (3, 3), (1, 3), (3, 1),
    (2, 1), (1, 2), (2, 3), (3, 2), (0, 2), (2, 0), (2, 2),
)


def exchange_kernel(pieces, decoded, out, send_sem, recv_sem, keep_sem):
    me_dir, me = lax.axis_index("dir"), lax.axis_index("row")
    core = lax.rem(me, 2)
    chip = me // 2
    x, y = chip // 4, lax.rem(chip, 4)
    each = decoded.shape[0] // 16
    lanes = decoded.shape[2]

    def chip_at(dx, dy):
        return lax.rem(x + dx, 4) * 4 + lax.rem(y + dy, 4)

    barrier = pltpu.get_barrier_semaphore()
    for dx, dy in AROUND:
        pl.semaphore_signal(
            barrier, inc=1, device_id=(me_dir, chip_at(dx, dy) * 2 + core), device_id_type=MESH
        )
    pl.semaphore_wait(barrier, len(AROUND))

    columns = pl.ds(pl.multiple_of(chip * lanes, 128), lanes)
    keep = pltpu.make_async_copy(decoded.at[pl.ds(chip * each, each)], out.at[:, :, columns], keep_sem)
    keep.start()
    size = each // pieces

    def copy(n, piece, order):
        dx, dy = AROUND[n] if order == 0 else AROUND[n][::-1]
        there = chip_at(dx, dy)
        return pltpu.make_async_remote_copy(
            src_ref=decoded.at[pl.ds(there * each + piece * size, size)],
            dst_ref=out.at[pl.ds(piece * size, size), :, columns],
            send_sem=send_sem.at[n, piece], recv_sem=recv_sem.at[n, piece],
            device_id=(me_dir, there * 2 + core), device_id_type=MESH,
        )

    for order in range(2):
        @pl.when(core == order)
        def _(order=order):
            for piece in range(pieces):
                for n in range(len(AROUND)):
                    copy(n, piece, order).start()

    keep.wait()
    for piece in range(pieces):
        for n in range(len(AROUND)):
            copy(n, piece, 0).wait()


def shards(influence, foot_rows, foot_columns, actuator_codes, poke_rows, subaperture_valid):
    mirrors, shard_rows, columns, slots = influence.shape
    n_dir, n_row = lax.axis_size("dir"), lax.axis_size("row")
    surface_rows = shard_rows * n_row
    me_dir, me = lax.axis_index("dir"), lax.axis_index("row")
    core, chip = me % 2, me // 2
    chip_rows = 2 * shard_rows
    first_row = chip * chip_rows - REACH
    subs = subaperture_valid.shape[2]
    acts = actuator_codes.size
    n_poke = poke_rows.shape[0]
    each = acts // (n_dir * n_row)
    mine = 16 * each
    wide = 256

    later, first = foot_columns[0, :, 1::2], foot_columns[0, :, 0::2]

    def windows(index):
        both = jnp.concatenate([index, index], axis=1)
        return jnp.stack(
            [jnp.pad(both, ((0, 0), (32 * i, 96 - 32 * i)), constant_values=-1) for i in range(4)],
            axis=1,
        )

    cols = jnp.concatenate([windows(later), windows(first)], axis=1).reshape(mirrors * 8, wide)
    valid = jnp.broadcast_to(subaperture_valid[0][:, None, :], (shard_rows // 2, 2, subs)).reshape(-1)
    window_rows = chip_rows + 2 * REACH
    local_rows = jnp.clip(foot_rows[0] - first_row, 0, window_rows - 1).reshape(-1)
    feet = jnp.concatenate(
        [valid, jnp.zeros((64,), jnp.int32), local_rows, jnp.zeros((116,), jnp.int32)]
    ).reshape(1, 512)

    def band_of(row):
        return jnp.clip(row * NAR // surface_rows - 1, 0, NAR - BAND)

    band_base = jnp.clip(first_row * NAR // surface_rows - 1, 0, NAR - SPAN)
    place = (band_of(first_row + jnp.arange(window_rows, dtype=jnp.int32)) - band_base) * NA
    place = jnp.clip(place, 0, (SPAN - BAND) * NA)
    mine_codes = lax.dynamic_slice(
        actuator_codes.reshape(n_dir, 16, 2, each), (me_dir, 0, core, 0), (1, 16, 1, each)
    ).reshape(mine, 1)
    local_codes = lax.dynamic_slice_in_dim(actuator_codes, band_base, SPAN, axis=1).reshape(1, -1)
    n_local = mirrors * SPAN * NA
    own = influence.transpose(0, 1, 3, 2)

    bf16, i32, f32 = jnp.bfloat16, jnp.int32, jnp.float32
    dma = pltpu.SemaphoreType.DMA
    gram, partner, above, below, all_feet, all_cols = pl.pallas_call(
        functools.partial(gram_kernel, n_dir, n_row),
        out_shape=(
            jax.ShapeDtypeStruct((mine, n_local), bf16),
            jax.ShapeDtypeStruct(own.shape, bf16),
            jax.ShapeDtypeStruct((mirrors, REACH, slots, columns), bf16),
            jax.ShapeDtypeStruct((mirrors, REACH, slots, columns), bf16),
            jax.ShapeDtypeStruct((2, n_dir, 1, 512), i32),
            jax.ShapeDtypeStruct((n_dir, mirrors * 8, wide), i32),
        ),
        in_specs=[VMEM, VMEM, VMEM, VMEM, ANY, ANY, ANY],
        out_specs=(VMEM, ANY, ANY, ANY, ANY, ANY),
        scratch_shapes=[
            pltpu.VMEM((mine, n_poke), bf16),
            pltpu.VMEM((n_poke, n_local), bf16),
            dma((2,)), dma((2,)), dma, dma,
            dma((n_dir, 2)), dma((n_dir, 2)), dma((n_dir,)), dma((n_dir,)),
        ],
        compiler_params=pltpu.CompilerParams(
            collective_id=0, has_side_effects=True, vmem_limit_bytes=48 << 20
        ),
        name="gram",
    )(mine_codes, poke_rows.reshape(1, -1), poke_rows.reshape(-1, 1), local_codes, own, feet, cols)

    lanes = 2 * (shard_rows // 2) * 2 * subs
    scale = 0.5 * n_poke ** (-0.5)
    mask = all_feet[:, :, 0, : lanes // 2].transpose(1, 0, 2).reshape(n_dir, lanes)
    mask = mask.astype(f32) * scale
    decoded = pl.pallas_call(
        apply_kernel,
        out_shape=jax.ShapeDtypeStruct((mine, n_dir, lanes), bf16),
        in_specs=[SMEM, SMEM, VMEM, ANY, ANY, ANY, ANY, VMEM, VMEM],
        out_specs=VMEM,
        scratch_shapes=[
            pltpu.VMEM((mirrors, window_rows, slots, columns), bf16),
            pltpu.VMEM((n_local, lanes), f32),
            pltpu.VMEM((n_local, lanes), bf16),
            pltpu.VMEM((lanes // 128, mine * n_dir, 128), f32),
            dma((4,)),
        ],
        compiler_params=pltpu.CompilerParams(vmem_limit_bytes=56 << 20),
        name="apply",
    )(all_feet, place, gram, own, partner, above, below, all_cols, mask)

    pieces = 3
    return pl.pallas_call(
        functools.partial(exchange_kernel, pieces),
        out_shape=jax.ShapeDtypeStruct((each, n_dir, lanes * 16), bf16),
        in_specs=[ANY],
        out_specs=ANY,
        scratch_shapes=[dma((15, pieces)), dma((15, pieces)), dma],
        compiler_params=pltpu.CompilerParams(collective_id=1, has_side_effects=True),
        name="exchange",
    )(decoded)


def solution(mesh):
    return jax.shard_map(
        shards,
        mesh=mesh,
        in_specs=(
            P(None, "row", None, None),
            P("dir", None, "row"),
            P("dir", None, None),
            P(),
            P(),
            P("dir", "row", None),
        ),
        out_specs=P(("dir", "row"), None, None),
        check_vma=False,
    )
```

```python
import functools

import jax
import jax.numpy as jnp
from jax import lax
from jax.experimental import pallas as pl
from jax.experimental.pallas import tpu as pltpu
from jax.sharding import PartitionSpec as P

NAR = 48
NA = 48
BAND = 3
REACH = 2
SPAN = 7
MESH = pl.DeviceIdType.MESH
ANY = pl.BlockSpec(memory_space=pl.ANY)
VMEM = pl.BlockSpec(memory_space=pltpu.VMEM)
SMEM = pl.BlockSpec(memory_space=pltpu.SMEM)


def sign_of(code_values, row_values):
    odd = jnp.bitwise_and(lax.population_count(jnp.bitwise_and(code_values, row_values)), 1)
    return jnp.where(odd == 0, 1.0, -1.0).astype(jnp.bfloat16)


def gram_kernel(n_dir, n_row, mine, pokes_lane, pokes_col, local, own, feet, cols,
                gram, partner, above, below, all_feet, all_cols,
                left, right, halo_send, halo_recv, pair_send, pair_recv,
                feet_send, feet_recv, cols_send, cols_recv):
    me_dir, me = lax.axis_index("dir"), lax.axis_index("row")
    core = lax.rem(me, 2)
    chip = me - core

    def row_of(step):
        return lax.rem(me + step + n_row, n_row)

    def other_core():
        return chip + 1 - core

    barrier = pltpu.get_barrier_semaphore()
    up_from = lax.rem(chip - 1 + n_row, n_row)
    down_from = lax.rem(chip + 2, n_row)
    for source in (up_from, down_from):
        pl.semaphore_signal(barrier, inc=1, device_id=(me_dir, source), device_id_type=MESH)
    for hop in range(n_dir):
        there = lax.rem(me_dir + hop, n_dir)
        if hop:
            pl.semaphore_signal(barrier, inc=1, device_id=(there, me), device_id_type=MESH)
        pl.semaphore_signal(barrier, inc=1, device_id=(there, other_core()), device_id_type=MESH)
    pl.semaphore_wait(barrier, 2 * n_dir + 1)

    copies = []

    def send(src, dst, send_sem, recv_sem, target):
        copy = pltpu.make_async_remote_copy(
            src_ref=src, dst_ref=dst, send_sem=send_sem, recv_sem=recv_sem,
            device_id=target, device_id_type=MESH,
        )
        copy.start()
        copies.append(copy)

    rows = own.shape[1]
    next_chip = lax.rem(chip + 2, n_row)
    prev_chip = lax.rem(chip - 2 + n_row, n_row)

    def halo(k, slot, to_core):
        edge = own.at[:, pl.ds(rows - REACH, REACH)] if k == 0 else own.at[:, pl.ds(0, REACH)]
        landing = above if k == 0 else below
        target = (next_chip if k == 0 else prev_chip) + to_core
        return pltpu.make_async_remote_copy(
            src_ref=edge, dst_ref=landing, send_sem=halo_send.at[to_core], recv_sem=halo_recv.at[k],
            device_id=(me_dir, target), device_id_type=MESH,
        )

    @pl.when(core == 1)
    def _():
        for to_core in range(2):
            halo(0, 0, to_core).start()

    @pl.when(core == 0)
    def _():
        for to_core in range(2):
            halo(1, 0, to_core).start()

    send(own, partner, pair_send, pair_recv, (me_dir, other_core()))
    for hop in range(n_dir):
        there = lax.rem(me_dir + hop, n_dir)
        if hop:
            send(feet, all_feet.at[core, me_dir], feet_send.at[hop, 0], feet_recv.at[hop, 0], (there, me))
            send(cols, all_cols.at[me_dir], cols_send.at[hop], cols_recv.at[hop], (there, me))
        send(feet, all_feet.at[core, me_dir], feet_send.at[hop, 1], feet_recv.at[hop, 1],
             (there, other_core()))
    local_feet = pltpu.make_async_copy(feet, all_feet.at[core, me_dir], feet_send.at[0, 0])
    local_feet.start()
    local_cols = pltpu.make_async_copy(cols, all_cols.at[me_dir], cols_send.at[0])
    local_cols.start()

    n_mine, n_poke = left.shape
    tile = 48

    @pl.loop(0, n_mine // tile)
    def _(step):
        at = pl.ds(pl.multiple_of(step * tile, tile), tile)
        left[at, :] = sign_of(mine[at, :], pokes_lane[...])

    high = 128

    @pl.loop(0, n_poke // high)
    def _(step):
        at = pl.ds(pl.multiple_of(step * high, high), high)
        right[at, :] = sign_of(local[...], pokes_col[at, :])

    gram[...] = jnp.dot(left[...], right[...], preferred_element_type=jnp.float32).astype(gram.dtype)

    local_feet.wait()
    local_cols.wait()
    for copy in copies:
        copy.wait()

    @pl.when(core == 1)
    def _():
        for to_core in range(2):
            halo(0, 0, to_core).wait_send()

    @pl.when(core == 0)
    def _():
        for to_core in range(2):
            halo(1, 0, to_core).wait_send()

    halo(0, 0, 0).wait_recv()
    halo(1, 0, 0).wait_recv()


AROUND = (
    (0, 1), (1, 0), (0, 3), (3, 0), (1, 1), (3, 3), (1, 3), (3, 1),
    (2, 1), (1, 2), (2, 3), (3, 2), (0, 2), (2, 0), (2, 2),
)
PLACE = tuple((3 * w - 6) // 8 + 1 for w in range(12))
REACHED = ((0, 5), (1, 4), (1, 5), (2, 5))


def deliver_kernel(chips, feet, gram, own, partner, above, below, cols, mask, out,
                   window, frames, sums, weights, staged, ready,
                   load_sem, send_sem, recv_sem, keep_sem):
    me_dir, me = lax.axis_index("dir"), lax.axis_index("row")
    core = lax.rem(me, 2)
    chip = lax.div(me, 2)
    x, y = lax.div(chip, 4), lax.rem(chip, 4)
    rows = own.shape[1]
    loads = [
        pltpu.make_async_copy(above, window.at[:, pl.ds(0, REACH)], load_sem.at[0]),
        pltpu.make_async_copy(own, window.at[:, pl.ds(REACH + rows * core, rows)], load_sem.at[1]),
        pltpu.make_async_copy(partner, window.at[:, pl.ds(REACH + rows * (1 - core), rows)], load_sem.at[2]),
        pltpu.make_async_copy(below, window.at[:, pl.ds(REACH + 2 * rows, REACH)], load_sem.at[3]),
    ]
    for load in loads:
        load.start()

    def chip_at(dx, dy):
        return lax.rem(x + dx, 4) * 4 + lax.rem(y + dy, 4)

    barrier = pltpu.get_barrier_semaphore()
    for dx, dy in AROUND:
        pl.semaphore_signal(
            barrier, inc=1, device_id=(me_dir, chip_at(dx, dy) * 2 + core), device_id_type=MESH
        )

    n_dir = mask.shape[0]
    mirrors, window_rows, slots, columns = window.shape
    frame = frames.shape[2]
    wide = cols.shape[-1]
    lanes = out.shape[2] // chips
    each = out.shape[0]
    lane = lax.broadcasted_iota(jnp.int32, (1, wide), 1)
    col_id = lax.broadcasted_iota(jnp.int32, (columns, wide), 0)

    frames[...] = jnp.zeros_like(frames)
    sums[...] = jnp.zeros_like(sums)
    for load in loads:
        load.wait()
    for w in range(window_rows):
        start = PLACE[w]
        if 2 <= w <= 4:
            start = start + 1 - lax.div(chip + chips - 1, chips)
        if 8 <= w <= 9:
            start = start - lax.div(chip + 1, chips)
        at = pl.ds(start * NA if isinstance(start, int) else pl.multiple_of(start * NA, NA), slots)
        for k in range(mirrors):
            frames[k, w, at, :] = window[k, w]

    def copy(n, t, order):
        dx, dy = AROUND[n] if order == 0 else AROUND[n][::-1]
        there = chip_at(dx, dy)
        return pltpu.make_async_remote_copy(
            src_ref=ready.at[t, pl.ds(there * each, each)],
            dst_ref=out.at[:, :, pl.ds(pl.multiple_of(chip * lanes + 128 * t, 128), 128)],
            send_sem=send_sem.at[n, t], recv_sem=recv_sem.at[n, t],
            device_id=(me_dir, there * 2 + core), device_id_type=MESH,
        )

    def keep(t):
        return pltpu.make_async_copy(
            ready.at[t, pl.ds(chip * each, each)],
            out.at[:, :, pl.ds(pl.multiple_of(chip * lanes + 128 * t, 128), 128)],
            keep_sem.at[t],
        )

    tiles = lanes // 128
    for t in range(tiles):
        if t < tiles - 1:
            low, many = REACHED[t]

            @pl.loop(0, n_dir)
            def _(d, t=t, low=low, many=many):
                block = pl.ds(pl.multiple_of(d * 128, 128), 128)
                for k in range(mirrors):
                    later = cols[d, 8 * k + t, :][None, :]
                    first = cols[d, 8 * k + 4 + t, :][None, :]
                    turn = jnp.where(lane < 32 * t + 80, -1.0, 1.0)
                    odd = jnp.where(col_id == later, 1.0, 0.0) + jnp.where(col_id == first, turn, 0.0)
                    even = odd * (-turn)
                    part = None
                    for a in range(2):
                        y = 2 * t + a
                        w = feet[y // rows, d, 0, 384 + rows * k + y % rows]
                        term = jnp.dot(
                            frames[k, w, pl.ds(low * NA, many * NA), :],
                            (odd if a else even).astype(jnp.bfloat16),
                            preferred_element_type=jnp.float32,
                        )
                        part = term if part is None else part + term
                    mine = pl.ds(k * frame + low * NA, many * NA)
                    whole = pl.ds(k * frame, frame)
                    sums[mine, block] += part[:, :128]
                    weights[whole, block] = sums[whole, block].astype(jnp.bfloat16)
                    sums[whole, block] = jnp.zeros((frame, 128), jnp.float32)
                    sums[mine, block] = part[:, 128:]
        else:
            weights[...] = sums[...].astype(jnp.bfloat16)

        @pl.loop(0, n_dir // 2)
        def _(c, t=t):
            part = jnp.dot(
                gram[...], weights[:, pl.ds(pl.multiple_of(c * 256, 256), 256)],
                preferred_element_type=jnp.float32,
            )
            for e in range(2):
                d = 2 * c + e
                scale = mask[d, t, :][None, :]
                staged[pl.ds(d, gram.shape[0], stride=n_dir), :] = part[:, 128 * e : 128 * (e + 1)] * scale

        @pl.loop(0, chips)
        def _(b, t=t):
            block = staged[pl.ds(pl.multiple_of(b * each * n_dir, n_dir), each * n_dir), :]
            ready[t, pl.ds(b * each, each)] = block.reshape(each, n_dir, 128).astype(ready.dtype)

        if t == 0:
            pl.semaphore_wait(barrier, len(AROUND))
        for order in range(2):
            @pl.when(core == order)
            def _(order=order, t=t):
                for n in range(len(AROUND)):
                    copy(n, t, order).start()
        keep(t).start()

    for t in range(tiles):
        keep(t).wait()
        for n in range(len(AROUND)):
            copy(n, t, 0).wait()


def shards(influence, foot_rows, foot_columns, actuator_codes, poke_rows, subaperture_valid):
    mirrors, shard_rows, columns, slots = influence.shape
    n_dir, n_row = lax.axis_size("dir"), lax.axis_size("row")
    me_dir, me = lax.axis_index("dir"), lax.axis_index("row")
    core, chip = me % 2, me // 2
    chip_rows = 2 * shard_rows
    first_row = chip * chip_rows - REACH
    subs = subaperture_valid.shape[2]
    acts = actuator_codes.size
    n_poke = poke_rows.shape[0]
    each = acts // (n_dir * n_row)
    mine = 16 * each
    wide = 256

    later, first = foot_columns[0, :, 1::2], foot_columns[0, :, 0::2]

    def windows(index):
        both = jnp.concatenate([index, index], axis=1)
        return jnp.stack(
            [jnp.pad(both, ((0, 0), (32 * i, 96 - 32 * i)), constant_values=-1) for i in range(4)],
            axis=1,
        )

    cols = jnp.concatenate([windows(later), windows(first)], axis=1).reshape(mirrors * 8, wide)
    valid = jnp.broadcast_to(subaperture_valid[0][:, None, :], (shard_rows // 2, 2, subs)).reshape(-1)
    window_rows = chip_rows + 2 * REACH
    local_rows = jnp.clip(foot_rows[0] - first_row, 0, window_rows - 1).reshape(-1)
    feet = jnp.concatenate(
        [valid, jnp.zeros((64,), jnp.int32), local_rows, jnp.zeros((116,), jnp.int32)]
    ).reshape(1, 512)

    chips = n_row // 2
    padded = jnp.pad(actuator_codes, ((0, 0), (2, 2), (0, 0)))
    mine_codes = lax.dynamic_slice(
        actuator_codes.reshape(n_dir, 16, 2, each), (me_dir, 0, core, 0), (1, 16, 1, each)
    ).reshape(mine, 1)
    local_codes = lax.dynamic_slice_in_dim(padded, 3 * chip, SPAN, axis=1).reshape(1, -1)
    n_local = mirrors * SPAN * NA
    own = influence.transpose(0, 1, 3, 2)

    bf16, i32, f32 = jnp.bfloat16, jnp.int32, jnp.float32
    dma = pltpu.SemaphoreType.DMA
    gram, partner, above, below, all_feet, all_cols = pl.pallas_call(
        functools.partial(gram_kernel, n_dir, n_row),
        out_shape=(
            jax.ShapeDtypeStruct((mine, n_local), bf16),
            jax.ShapeDtypeStruct(own.shape, bf16),
            jax.ShapeDtypeStruct((mirrors, REACH, slots, columns), bf16),
            jax.ShapeDtypeStruct((mirrors, REACH, slots, columns), bf16),
            jax.ShapeDtypeStruct((2, n_dir, 1, 512), i32),
            jax.ShapeDtypeStruct((n_dir, mirrors * 8, wide), i32),
        ),
        in_specs=[VMEM, VMEM, VMEM, VMEM, ANY, ANY, ANY],
        out_specs=(VMEM, ANY, ANY, ANY, ANY, ANY),
        scratch_shapes=[
            pltpu.VMEM((mine, n_poke), bf16),
            pltpu.VMEM((n_poke, n_local), bf16),
            dma((2,)), dma((2,)), dma, dma,
            dma((n_dir, 2)), dma((n_dir, 2)), dma((n_dir,)), dma((n_dir,)),
        ],
        compiler_params=pltpu.CompilerParams(
            collective_id=0, has_side_effects=True
        ),
        name="gram",
    )(mine_codes, poke_rows.reshape(1, -1), poke_rows.reshape(-1, 1), local_codes, own, feet, cols)

    lanes = 2 * (shard_rows // 2) * 2 * subs
    scale = 0.5 * n_poke ** (-0.5)
    mask = all_feet[:, :, 0, : lanes // 2].transpose(1, 0, 2).reshape(n_dir, lanes)
    mask = (mask.astype(f32) * scale).reshape(n_dir, lanes // 128, 128)
    tiles = lanes // 128
    return pl.pallas_call(
        functools.partial(deliver_kernel, chips),
        out_shape=jax.ShapeDtypeStruct((each, n_dir, lanes * chips), bf16),
        in_specs=[SMEM, VMEM, ANY, ANY, ANY, ANY, VMEM, VMEM],
        out_specs=ANY,
        scratch_shapes=[
            pltpu.VMEM((mirrors, window_rows, slots, columns), bf16),
            pltpu.VMEM((mirrors, window_rows, SPAN * NA, columns), bf16),
            pltpu.VMEM((n_local, n_dir * 128), f32),
            pltpu.VMEM((n_local, n_dir * 128), bf16),
            pltpu.VMEM((mine * n_dir, 128), f32),
            pltpu.VMEM((tiles, mine, n_dir, 128), bf16),
            dma((4,)), dma((15, tiles)), dma((15, tiles)), dma((tiles,)),
        ],
        compiler_params=pltpu.CompilerParams(collective_id=1, has_side_effects=True),
        name="deliver",
    )(all_feet, gram, own, partner, above, below, all_cols, mask)


def solution(mesh):
    return jax.shard_map(
        shards,
        mesh=mesh,
        in_specs=(
            P(None, "row", None, None),
            P("dir", None, "row"),
            P("dir", None, None),
            P(),
            P(),
            P("dir", "row", None),
        ),
        out_specs=P(("dir", "row"), None, None),
        check_vma=False,
    )
```

```python
import functools

import jax
import jax.numpy as jnp
from jax import lax
from jax.experimental import pallas as pl
from jax.experimental.pallas import tpu as pltpu
from jax.sharding import PartitionSpec as P

NAR = 48
NA = 48
REACH = 2
SPAN = 7
MESH = pl.DeviceIdType.MESH
ANY = pl.BlockSpec(memory_space=pl.ANY)
VMEM = pl.BlockSpec(memory_space=pltpu.VMEM)

AROUND = (
    (0, 1), (1, 0), (0, 3), (3, 0), (1, 1), (3, 3), (1, 3), (3, 1),
    (2, 1), (1, 2), (2, 3), (3, 2), (0, 2), (2, 0), (2, 2),
)
PLACE = tuple((3 * w - 6) // 8 + 1 for w in range(12))
REACHED = ((0, 5), (1, 4), (1, 5), (2, 5))
BF16, F32, I32 = jnp.bfloat16, jnp.float32, jnp.int32


def iota(shape, axis):
    return lax.broadcasted_iota(I32, shape, axis)


def over(value, divisor):
    return jnp.right_shift(value * (65536 // divisor + 1), 16)


def sign_of(code_values, row_values):
    odd = jnp.bitwise_and(lax.population_count(jnp.bitwise_and(code_values, row_values)), 1)
    return jnp.where(odd == 0, 1.0, -1.0).astype(BF16)


def dot(a, b):
    return jnp.dot(a, b, preferred_element_type=F32)


def halves(codes):
    return jnp.right_shift(codes, 7).astype(F32).astype(BF16), jnp.bitwise_and(codes, 127).astype(F32).astype(BF16)


def window_kernel(n_dir, n_row, own, foot_rows, foot_cols, valid, codes, pokes_lane, pokes_tile, out,
                  window, frames, sums, weights, staged, ready, left, right, gram, mine, local,
                  feet_land, cols_land, valid_land, feet, cols_mat, valid_mat, picks, mask,
                  far_send, far_recv, halo_send, halo_recv, pair_send, pair_recv,
                  feet_send, feet_recv, cols_send, cols_recv, valid_send, valid_recv, keep_sem, own_sem):
    me_dir, me = lax.axis_index("dir"), lax.axis_index("row")
    core = lax.rem(me, 2)
    chip = lax.div(me, 2)
    chips = n_row // 2
    x, y = lax.div(chip, 4), lax.rem(chip, 4)
    rows = own.shape[1]
    mirrors, window_rows, slots, columns = window.shape
    frame = frames.shape[2]
    lanes = out.shape[2] // chips
    each = out.shape[0]
    tiles = lanes // 128

    def chip_at(dx, dy):
        return lax.rem(x + dx, 4) * 4 + lax.rem(y + dy, 4)

    barrier = pltpu.get_barrier_semaphore()

    def greet(there_dir, there):
        pl.semaphore_signal(barrier, inc=1, device_id=(there_dir, there), device_id_type=MESH)

    greet(me_dir, lax.rem(2 * chip - 1 + n_row, n_row))
    greet(me_dir, lax.rem(2 * chip + 2, n_row))
    for hop in range(n_dir):
        there = lax.rem(me_dir + hop, n_dir)
        if hop:
            greet(there, me)
        greet(there, 2 * chip + 1 - core)
    for dx, dy in AROUND:
        greet(me_dir, chip_at(dx, dy) * 2 + core)

    keeps = [
        pltpu.make_async_copy(own, window.at[:, pl.ds(REACH + rows * core, rows)], own_sem.at[0]),
        pltpu.make_async_copy(foot_rows, feet_land.at[core * n_dir + me_dir], own_sem.at[1]),
        pltpu.make_async_copy(foot_cols, cols_land.at[me_dir], own_sem.at[2]),
        pltpu.make_async_copy(valid, valid_land.at[core * n_dir + me_dir], own_sem.at[3]),
    ]
    for copy in keeps:
        copy.start()

    pl.semaphore_wait(barrier, 2 * n_dir - 1 + 2 + len(AROUND))

    def remote(src, dst, send_sem, recv_sem, target):
        return pltpu.make_async_remote_copy(
            src_ref=src, dst_ref=dst, send_sem=send_sem, recv_sem=recv_sem,
            device_id=target, device_id_type=MESH,
        )

    def halo(k, to_core):
        edge = own.at[:, pl.ds(rows - REACH, REACH)] if k == 0 else own.at[:, pl.ds(0, REACH)]
        landing = window.at[:, pl.ds(0 if k == 0 else REACH + 2 * rows, REACH)]
        target = lax.rem(2 * chip + (2 if k == 0 else n_row - 2), n_row)
        return remote(edge, landing, halo_send.at[to_core], halo_recv.at[k], (me_dir, target + to_core))

    @pl.when(core == 1)
    def _():
        for to_core in range(2):
            halo(0, to_core).start()

    @pl.when(core == 0)
    def _():
        for to_core in range(2):
            halo(1, to_core).start()

    pair = remote(own, window.at[:, pl.ds(REACH + rows * core, rows)], pair_send, pair_recv,
                  (me_dir, 2 * chip + 1 - core))
    pair.start()
    small = []
    for hop in range(n_dir):
        there = lax.rem(me_dir + hop, n_dir)
        for side in range(2):
            if hop == 0 and side == 0:
                continue
            target = (there, me if side == 0 else 2 * chip + 1 - core)
            small.append(remote(foot_rows, feet_land.at[core * n_dir + me_dir],
                                feet_send.at[hop, side], feet_recv.at[hop, side], target))
            small.append(remote(valid, valid_land.at[core * n_dir + me_dir],
                                valid_send.at[hop, side], valid_recv.at[hop, side], target))
        if hop:
            small.append(remote(foot_cols, cols_land.at[me_dir], cols_send.at[hop], cols_recv.at[hop],
                                (there, me)))
    for copy in small:
        copy.start()

    n_mine, n_poke = left.shape
    n_local = right.shape[1]
    table = [halves(codes[k]) for k in range(mirrors)]
    at = iota((n_mine, 1), 0)
    at = at + each * (over(at, each) + core)
    at_row = over(at, NA)
    at_col = at - NA * at_row
    per_dir = mirrors * NAR // n_dir
    upper = jnp.zeros((n_mine, NA), F32)
    lower = jnp.zeros((n_mine, NA), F32)
    for k in range(mirrors):
        hot = (iota((n_mine, NAR), 1) == at_row + (per_dir * me_dir - NAR * k)).astype(F32).astype(BF16)
        upper += dot(hot, table[k][0])
        lower += dot(hot, table[k][1])
    picked = jnp.where(iota((n_mine, NA), 1) == at_col, upper * 128.0 + lower, 0.0)
    mine[...] = jnp.sum(picked, axis=1, keepdims=True).astype(I32)

    lane = iota((1, n_local), 1)
    block = over(lane, NA)
    tile_of = (iota((NA, n_local), 0) == lane - NA * block).astype(F32).astype(BF16)
    row_id = iota((NAR, n_local), 0)
    found = jnp.zeros((1, n_local), F32)
    for k in range(mirrors):
        spread = dot(table[k][0], tile_of) * 128.0 + dot(table[k][1], tile_of)
        wanted = jnp.where((block >= SPAN * k) & (block < SPAN * (k + 1)), block - SPAN * k + 3 * chip - 2, -1)
        found += jnp.sum(jnp.where(row_id == wanted, spread, 0.0), axis=0, keepdims=True)
    local[...] = found.astype(I32)

    turned = jnp.transpose(pokes_tile[...])
    for j in range(n_poke // 128):
        right[128 * j : 128 * (j + 1), :] = sign_of(turned[:, j : j + 1], local[...])

    @pl.loop(0, n_mine // 48)
    def _(step):
        part = pl.ds(pl.multiple_of(step * 48, 48), 48)
        left[part, :] = sign_of(mine[part, :], pokes_lane[...])

    gram[...] = dot(left[...], right[...]).astype(BF16)

    for copy in keeps:
        copy.wait()
    for copy in small:
        copy.wait()
    to_scalar = pltpu.make_async_copy(feet_land, feet, own_sem.at[4])
    to_scalar.start()
    for d in range(n_dir):
        for k in range(mirrors):
            cols_mat[d * mirrors + k : d * mirrors + k + 1, :] = cols_land[d, k]
        for i in range(rows):
            valid_mat[i, d : d + 1, :] = valid_land[i // 2 * n_dir + d, 0, i % 2 : i % 2 + 1, :]
    n_cols = cols_mat.shape[1]
    subs = n_cols // 2
    wide = picks.shape[2]
    cols_value = cols_mat[...].astype(F32).astype(BF16)
    for t in range(4):
        lane = iota((1, wide), 1) - 32 * t
        inside = (lane >= 0) & (lane < n_cols)
        column = 2 * jnp.where(lane >= subs, lane - subs, lane)
        for first in range(2):
            wanted = jnp.where(inside, column + 1 - first, -1)
            hot = (iota((n_cols, wide), 0) == wanted).astype(F32).astype(BF16)
            value = jnp.where(inside, dot(cols_value, hot), -1.0)
            for r in range(n_dir * mirrors):
                picks[(4 * first + t) * n_dir * mirrors + r] = value[r : r + 1, :]
    lane = iota((1, lanes), 1)
    hot = (iota((subs, lanes), 0) == lane - subs * over(lane, subs)).astype(F32).astype(BF16)
    total = jnp.zeros((n_dir, lanes), F32)
    for i in range(rows):
        value = dot(valid_mat[i].astype(F32).astype(BF16), hot)
        total += jnp.where((lane >= n_cols * i) & (lane < n_cols * (i + 1)), value, 0.0)
    total = total * (0.5 * n_poke ** (-0.5))
    for t in range(tiles):
        for d in range(n_dir):
            mask[t * n_dir + d] = total[d : d + 1, 128 * t : 128 * (t + 1)]

    frames[...] = jnp.zeros_like(frames)
    sums[...] = jnp.zeros_like(sums)
    to_scalar.wait()
    pair.wait()

    @pl.when(core == 1)
    def _():
        for to_core in range(2):
            halo(0, to_core).wait_send()

    @pl.when(core == 0)
    def _():
        for to_core in range(2):
            halo(1, to_core).wait_send()

    halo(0, 0).wait_recv()
    halo(1, 0).wait_recv()
    for w in range(window_rows):
        start = PLACE[w]
        if 2 <= w <= 4:
            start = start + 1 - lax.div(chip + chips - 1, chips)
        if 8 <= w <= 9:
            start = start - lax.div(chip + 1, chips)
        part = pl.ds(start * NA if isinstance(start, int) else pl.multiple_of(start * NA, NA), slots)
        for k in range(mirrors):
            frames[k, w, part, :] = window[k, w]

    def far(n, t, order):
        dx, dy = AROUND[n] if order == 0 else AROUND[n][::-1]
        there = chip_at(dx, dy)
        return remote(
            ready.at[t, pl.ds(there * each, each)],
            out.at[:, :, pl.ds(pl.multiple_of(chip * lanes + 128 * t, 128), 128)],
            far_send.at[n, t], far_recv.at[n, t], (me_dir, there * 2 + core),
        )

    def keep(t):
        return pltpu.make_async_copy(
            ready.at[t, pl.ds(chip * each, each)],
            out.at[:, :, pl.ds(pl.multiple_of(chip * lanes + 128 * t, 128), 128)],
            keep_sem.at[t],
        )

    col_id = iota((columns, wide), 0).astype(F32)
    lane = iota((1, wide), 1)
    for t in range(tiles):
        if t < tiles - 1:
            low, many = REACHED[t]
            turn = jnp.where(lane < 32 * t + subs, -1.0, 1.0)

            @pl.loop(0, n_dir)
            def _(d, t=t, low=low, many=many, turn=turn):
                block = pl.ds(pl.multiple_of(d * 128, 128), 128)
                for k in range(mirrors):
                    later = picks[t * n_dir * mirrors + d * mirrors + k]
                    first = picks[(4 + t) * n_dir * mirrors + d * mirrors + k]
                    odd = jnp.where(col_id == later, 1.0, 0.0) + jnp.where(col_id == first, turn, 0.0)
                    even = odd * (-turn)
                    part = None
                    for a in range(2):
                        row = 2 * t + a
                        at = feet[row // rows * n_dir + d, k, 0, row % rows]
                        w = jnp.clip(at - 2 * rows * chip + REACH, 0, window_rows - 1)
                        term = dot(frames[k, w, pl.ds(low * NA, many * NA), :],
                                   (odd if a else even).astype(BF16))
                        part = term if part is None else part + term
                    some = pl.ds(k * frame + low * NA, many * NA)
                    whole = pl.ds(k * frame, frame)
                    sums[some, block] += part[:, :128]
                    weights[whole, block] = sums[whole, block].astype(BF16)
                    sums[whole, block] = jnp.zeros((frame, 128), F32)
                    sums[some, block] = part[:, 128:]
        else:
            weights[...] = sums[...].astype(BF16)

        @pl.loop(0, n_dir // 2)
        def _(c, t=t):
            part = dot(gram[...], weights[:, pl.ds(pl.multiple_of(c * 256, 256), 256)])
            for e in range(2):
                d = 2 * c + e
                staged[pl.ds(d, n_mine, stride=n_dir), :] = part[:, 128 * e : 128 * (e + 1)] * mask[t * n_dir + d]

        @pl.loop(0, chips)
        def _(b, t=t):
            block = staged[pl.ds(pl.multiple_of(b * each * n_dir, n_dir), each * n_dir), :]
            ready[t, pl.ds(b * each, each)] = block.reshape(each, n_dir, 128).astype(BF16)

        for order in range(2):
            @pl.when(core == order)
            def _(order=order, t=t):
                for n in range(len(AROUND)):
                    far(n, t, order).start()
        keep(t).start()

    for t in range(tiles):
        keep(t).wait()
        for n in range(len(AROUND)):
            far(n, t, 0).wait()


def shards(influence, foot_rows, foot_columns, actuator_codes, poke_rows, subaperture_valid):
    mirrors, shard_rows, columns, slots = influence.shape
    n_dir, n_row = lax.axis_size("dir"), lax.axis_size("row")
    chips = n_row // 2
    window_rows = 2 * shard_rows + 2 * REACH
    subs = subaperture_valid.shape[2]
    n_poke = poke_rows.shape[0]
    each = actuator_codes.size // (n_dir * n_row)
    n_mine = chips * each
    n_local = mirrors * SPAN * NA
    lanes = 2 * shard_rows * subs
    tiles = lanes // 128
    dma = pltpu.SemaphoreType.DMA
    return pl.pallas_call(
        functools.partial(window_kernel, n_dir, n_row),
        out_shape=jax.ShapeDtypeStruct((each, n_dir, lanes * chips), BF16),
        in_specs=[ANY, ANY, ANY, ANY, VMEM, VMEM, VMEM],
        out_specs=ANY,
        scratch_shapes=[
            pltpu.VMEM((mirrors, window_rows, slots, columns), BF16),
            pltpu.VMEM((mirrors, window_rows, SPAN * NA, columns), BF16),
            pltpu.VMEM((n_local, n_dir * 128), F32),
            pltpu.VMEM((n_local, n_dir * 128), BF16),
            pltpu.VMEM((n_mine * n_dir, 128), F32),
            pltpu.VMEM((tiles, n_mine, n_dir, 128), BF16),
            pltpu.VMEM((n_mine, n_poke), BF16),
            pltpu.VMEM((n_poke, n_local), BF16),
            pltpu.VMEM((n_mine, n_local), BF16),
            pltpu.VMEM((n_mine, 1), I32),
            pltpu.VMEM((1, n_local), I32),
            pltpu.VMEM((2 * n_dir, mirrors, 1, shard_rows), I32),
            pltpu.VMEM((n_dir, mirrors, 1, 2 * subs), I32),
            pltpu.VMEM((2 * n_dir, 1, shard_rows // 2, subs), I32),
            pltpu.SMEM((2 * n_dir, mirrors, 1, shard_rows), I32),
            pltpu.VMEM((n_dir * mirrors, 2 * subs), I32),
            pltpu.VMEM((shard_rows, n_dir, subs), I32),
            pltpu.VMEM((8 * n_dir * mirrors, 1, 256), F32),
            pltpu.VMEM((tiles * n_dir, 1, 128), F32),
            dma((15, tiles)), dma((15, tiles)), dma((2,)), dma((2,)), dma, dma,
            dma((n_dir, 2)), dma((n_dir, 2)), dma((n_dir,)), dma((n_dir,)),
            dma((n_dir, 2)), dma((n_dir, 2)), dma((tiles,)), dma((5,)),
        ],
        compiler_params=pltpu.CompilerParams(collective_id=0, has_side_effects=True),
        name="window",
    )(
        influence.transpose(0, 1, 3, 2),
        foot_rows.reshape(mirrors, 1, shard_rows),
        foot_columns.reshape(mirrors, 1, 2 * subs),
        subaperture_valid,
        actuator_codes,
        poke_rows.reshape(1, -1),
        poke_rows.reshape(-1, 128),
    )


def solution(mesh):
    return jax.shard_map(
        shards,
        mesh=mesh,
        in_specs=(
            P(None, "row", None, None),
            P("dir", None, "row"),
            P("dir", None, None),
            P(),
            P(),
            P("dir", "row", None),
        ),
        out_specs=P(("dir", "row"), None, None),
        check_vma=False,
    )
```

```python
import functools

import jax
import jax.numpy as jnp
from jax import lax
from jax.experimental import pallas as pl
from jax.experimental.pallas import tpu as pltpu
from jax.sharding import PartitionSpec as P

NAR = 48
NA = 48
REACH = 2
SPAN = 7
MESH = pl.DeviceIdType.MESH
ANY = pl.BlockSpec(memory_space=pl.ANY)
VMEM = pl.BlockSpec(memory_space=pltpu.VMEM)

AROUND = (
    (0, 1), (1, 0), (0, 3), (3, 0), (1, 1), (3, 3), (1, 3), (3, 1),
    (2, 1), (1, 2), (2, 3), (3, 2), (0, 2), (2, 0), (2, 2),
)
PLACE = tuple((3 * w - 6) // 8 + 1 for w in range(12))
REACHED = ((0, 5), (1, 4), (1, 5), (2, 5))
BF16, F32, I32 = jnp.bfloat16, jnp.float32, jnp.int32


def iota(shape, axis):
    return lax.broadcasted_iota(I32, shape, axis)


def over(value, divisor):
    return jnp.right_shift(value * (65536 // divisor + 1), 16)


def sign_of(code_values, row_values):
    odd = jnp.bitwise_and(lax.population_count(jnp.bitwise_and(code_values, row_values)), 1)
    return jnp.where(odd == 0, 1.0, -1.0).astype(BF16)


def dot(a, b):
    return jnp.dot(a, b, preferred_element_type=F32)


def halves(codes):
    return jnp.right_shift(codes, 7).astype(F32).astype(BF16), jnp.bitwise_and(codes, 127).astype(F32).astype(BF16)


def window_kernel(n_dir, n_row, own, foot_rows, foot_cols, valid, codes, pokes_lane, pokes_tile, out,
                  window, frames, sums, weights, staged, ready, left, right, gram, mine, local,
                  feet_land, cols_land, valid_land, feet, cols_mat, valid_mat, picks, mask,
                  poke_cols, far_send, far_recv, halo_send, halo_recv, pair_send, pair_recv, relay_send, relay_recv,
                  feet_send, feet_recv, cols_send, cols_recv, valid_send, valid_recv, keep_sem, own_sem):
    me_dir, me = lax.axis_index("dir"), lax.axis_index("row")
    core = lax.rem(me, 2)
    chip = lax.div(me, 2)
    chips = n_row // 2
    x, y = lax.div(chip, 4), lax.rem(chip, 4)
    rows = own.shape[1]
    mirrors, window_rows, slots, columns = window.shape
    frame = frames.shape[2]
    lanes = out.shape[2] // chips
    each = out.shape[0]
    tiles = lanes // 128

    def chip_at(dx, dy):
        return lax.rem(x + dx, 4) * 4 + lax.rem(y + dy, 4)

    barrier = pltpu.get_barrier_semaphore()

    def greet(there_dir, there):
        pl.semaphore_signal(barrier, inc=1, device_id=(there_dir, there), device_id_type=MESH)

    beside = lax.rem(2 * chip + 3 * core - 1 + n_row, n_row)
    twin = 2 * chip + 1 - core
    greet(me_dir, beside)
    for hop in range(n_dir):
        there = lax.rem(me_dir + hop, n_dir)
        if hop:
            greet(there, me)
        greet(there, twin)
    for dx, dy in AROUND:
        greet(me_dir, chip_at(dx, dy) * 2 + core)

    keeps = [
        pltpu.make_async_copy(own, window.at[:, pl.ds(REACH + rows * core, rows)], own_sem.at[0]),
        pltpu.make_async_copy(foot_rows, feet_land.at[core * n_dir + me_dir], own_sem.at[1]),
        pltpu.make_async_copy(foot_cols, cols_land.at[me_dir], own_sem.at[2]),
        pltpu.make_async_copy(valid, valid_land.at[core * n_dir + me_dir], own_sem.at[3]),
    ]
    for copy in keeps:
        copy.start()

    n_mine, n_poke = left.shape
    n_local = right.shape[1]
    table = [halves(codes[k]) for k in range(mirrors)]
    at = iota((n_mine, 1), 0)
    at = at + each * (over(at, each) + core)
    at_row = over(at, NA)
    at_col = at - NA * at_row
    per_dir = mirrors * NAR // n_dir
    upper = jnp.zeros((n_mine, NA), F32)
    lower = jnp.zeros((n_mine, NA), F32)
    for k in range(mirrors):
        hot = (iota((n_mine, NAR), 1) == at_row + (per_dir * me_dir - NAR * k)).astype(F32).astype(BF16)
        upper += dot(hot, table[k][0])
        lower += dot(hot, table[k][1])
    picked = jnp.where(iota((n_mine, NA), 1) == at_col, upper * 128.0 + lower, 0.0)
    mine[...] = jnp.sum(picked, axis=1, keepdims=True).astype(I32)

    lane = iota((1, n_local), 1)
    block = over(lane, NA)
    tile_of = (iota((NA, n_local), 0) == lane - NA * block).astype(F32).astype(BF16)
    row_id = iota((NAR, n_local), 0)
    found = jnp.zeros((1, n_local), F32)
    for k in range(mirrors):
        spread = dot(table[k][0], tile_of) * 128.0 + dot(table[k][1], tile_of)
        wanted = jnp.where((block >= SPAN * k) & (block < SPAN * (k + 1)), block - SPAN * k + 3 * chip - 2, -1)
        found += jnp.sum(jnp.where(row_id == wanted, spread, 0.0), axis=0, keepdims=True)
    local[...] = found.astype(I32)

    turned = jnp.transpose(pokes_tile[...])
    for j in range(n_poke // 128):
        poke_cols[j] = turned[:, j : j + 1]
    frames[...] = jnp.zeros_like(frames)

    pl.semaphore_wait(barrier, 2 * n_dir + len(AROUND))

    def remote(src, dst, send_sem, recv_sem, target):
        return pltpu.make_async_remote_copy(
            src_ref=src, dst_ref=dst, send_sem=send_sem, recv_sem=recv_sem,
            device_id=target, device_id_type=MESH,
        )

    far_edge = REACH + 2 * rows
    halo = remote(own.at[:, pl.ds((rows - REACH) * core, REACH)],
                  window.at[:, pl.ds(far_edge * (1 - core), REACH)], halo_send, halo_recv, (me_dir, beside))
    halo.start()
    pair = [
        remote(own.at[k], window.at[k, pl.ds(REACH + rows * core, rows)], pair_send.at[k], pair_recv.at[k],
               (me_dir, twin))
        for k in range(mirrors)
    ]
    for copy in pair:
        copy.start()
    small = []
    for hop in range(n_dir):
        there = lax.rem(me_dir + hop, n_dir)
        for side in range(2):
            if hop == 0 and side == 0:
                continue
            target = (there, me if side == 0 else twin)
            small.append(remote(foot_rows, feet_land.at[core * n_dir + me_dir],
                                feet_send.at[hop, side], feet_recv.at[hop, side], target))
            small.append(remote(valid, valid_land.at[core * n_dir + me_dir],
                                valid_send.at[hop, side], valid_recv.at[hop, side], target))
        if hop:
            small.append(remote(foot_cols, cols_land.at[me_dir], cols_send.at[hop], cols_recv.at[hop],
                                (there, me)))
    for copy in small:
        copy.start()

    @pl.loop(0, n_poke // 128)
    def _(j):
        part = pl.ds(pl.multiple_of(j * 128, 128), 128)
        right[part, :] = sign_of(poke_cols[j], local[...])

    relay = remote(window.at[:, pl.ds(far_edge * core, REACH)], window.at[:, pl.ds(far_edge * core, REACH)],
                   relay_send, relay_recv, (me_dir, twin))

    @pl.loop(0, n_mine // 48)
    def _(step):
        part = pl.ds(pl.multiple_of(step * 48, 48), 48)
        left[part, :] = sign_of(mine[part, :], pokes_lane[...])

    gram[...] = dot(left[...], right[...]).astype(BF16)

    for copy in keeps:
        copy.wait()
    for copy in small:
        copy.wait()
    to_scalar = pltpu.make_async_copy(feet_land, feet, own_sem.at[4])
    to_scalar.start()
    for d in range(n_dir):
        for k in range(mirrors):
            cols_mat[d * mirrors + k : d * mirrors + k + 1, :] = cols_land[d, k]
        for i in range(rows):
            valid_mat[i, d : d + 1, :] = valid_land[i // 2 * n_dir + d, 0, i % 2 : i % 2 + 1, :]
    n_cols = cols_mat.shape[1]
    subs = n_cols // 2
    wide = picks.shape[2]
    def pick(t):
        lane = iota((1, wide), 1) - 32 * t
        inside = (lane >= 0) & (lane < n_cols)
        column = 2 * jnp.where(lane >= subs, lane - subs, lane)
        for first in range(2):
            wanted = jnp.where(inside, column + 1 - first, -1)
            hot = (iota((n_cols, wide), 0) == wanted).astype(F32).astype(BF16)
            value = jnp.where(inside, dot(cols_mat[...].astype(F32).astype(BF16), hot), -1.0)
            for r in range(n_dir * mirrors):
                picks[first * n_dir * mirrors + r] = value[r : r + 1, :]

    lane = iota((1, lanes), 1)
    hot = (iota((subs, lanes), 0) == lane - subs * over(lane, subs)).astype(F32).astype(BF16)
    total = jnp.zeros((n_dir, lanes), F32)
    for i in range(rows):
        value = dot(valid_mat[i].astype(F32).astype(BF16), hot)
        total += jnp.where((lane >= n_cols * i) & (lane < n_cols * (i + 1)), value, 0.0)
    total = total * (0.5 * n_poke ** (-0.5))
    for t in range(tiles):
        for d in range(n_dir):
            mask[t * n_dir + d] = total[d : d + 1, 128 * t : 128 * (t + 1)]

    to_scalar.wait()
    for copy in pair:
        copy.wait()

    def fill(some):
        for w in some:
            start = PLACE[w]
            if 2 <= w <= 4:
                start = start + 1 - lax.div(chip + chips - 1, chips)
            if 8 <= w <= 9:
                start = start - lax.div(chip + 1, chips)
            part = pl.ds(start * NA if isinstance(start, int) else pl.multiple_of(start * NA, NA), slots)
            for k in range(mirrors):
                frames[k, w, part, :] = window[k, w]

    fill(range(REACH, far_edge))

    def far(n, t, order):
        dx, dy = AROUND[n] if order == 0 else AROUND[n][::-1]
        there = chip_at(dx, dy)
        return remote(
            ready.at[t, pl.ds(there * each, each)],
            out.at[:, :, pl.ds(pl.multiple_of(chip * lanes + 128 * t, 128), 128)],
            far_send.at[n, t], far_recv.at[n, t], (me_dir, there * 2 + core),
        )

    def keep(t):
        return pltpu.make_async_copy(
            ready.at[t, pl.ds(chip * each, each)],
            out.at[:, :, pl.ds(pl.multiple_of(chip * lanes + 128 * t, 128), 128)],
            keep_sem.at[t],
        )

    col_id = iota((columns, wide), 0).astype(F32)
    lane = iota((1, wide), 1)
    def sample(i):
        low, many = REACHED[i]
        turn = jnp.where(lane < 32 * i + subs, -1.0, 1.0)
        pick(i)

        def framed(value):
            blank = [jnp.zeros((n * NA, 128), F32) for n in (low, SPAN - low - many)]
            pieces = [blank[0], value, blank[1]]
            return jnp.concatenate([p for p in pieces if p.shape[0]], axis=0)

        @pl.loop(0, n_dir)
        def _(d):
            block = pl.ds(pl.multiple_of(d * 128, 128), 128)
            for k in range(mirrors):
                later = picks[d * mirrors + k]
                first = picks[(n_dir + d) * mirrors + k]
                hot = jnp.where(col_id == later, 1.0, 0.0) + jnp.where(col_id == first, turn, 0.0)
                hot = hot.astype(BF16)
                terms = []
                for a in range(2):
                    row = 2 * i + a
                    at = feet[row // rows * n_dir + d, k, 0, row % rows]
                    w = jnp.clip(at - 2 * rows * chip + REACH, 0, window_rows - 1)
                    terms.append(dot(frames[k, w, pl.ds(low * NA, many * NA), :], hot))
                part = terms[1] - terms[0] * turn
                whole = pl.ds(k * frame, frame)
                here, after = framed(part[:, :128]), framed(part[:, 128:])
                if i == 1:
                    sums[0, whole, block] = here
                    sums[1, whole, block] = after
                elif i == 0:
                    weights[whole, block] = here.astype(BF16)
                    sums[0, whole, block] += after
                else:
                    weights[whole, block] = (here + sums[1, whole, block]).astype(BF16)
                    sums[1, whole, block] = after

    def deliver(t):
        @pl.loop(0, n_dir // 2)
        def _(c):
            part = dot(gram[...], weights[:, pl.ds(pl.multiple_of(c * 256, 256), 256)])
            for e in range(2):
                d = 2 * c + e
                staged[pl.ds(d, n_mine, stride=n_dir), :] = part[:, 128 * e : 128 * (e + 1)] * mask[t * n_dir + d]

        @pl.loop(0, chips)
        def _(b):
            block = staged[pl.ds(pl.multiple_of(b * each * n_dir, n_dir), each * n_dir), :]
            ready[t, pl.ds(b * each, each)] = block.reshape(each, n_dir, 128).astype(BF16)

        for order in range(2):
            @pl.when(core == order)
            def _(order=order):
                for n in range(len(AROUND)):
                    far(n, t, order).start()
        keep(t).start()

    sample(1)
    halo.wait()
    relay.start()
    sample(2)
    deliver(2)
    relay.wait()
    fill((0, 1, far_edge, far_edge + 1))
    sample(0)
    deliver(0)
    weights[...] = sums[0].astype(BF16)
    deliver(1)
    sample(3)
    deliver(3)
    weights[...] = sums[1].astype(BF16)
    deliver(4)

    for t in range(tiles):
        keep(t).wait()
        for n in range(len(AROUND)):
            far(n, t, 0).wait()


def shards(influence, foot_rows, foot_columns, actuator_codes, poke_rows, subaperture_valid):
    mirrors, shard_rows, columns, slots = influence.shape
    n_dir, n_row = lax.axis_size("dir"), lax.axis_size("row")
    chips = n_row // 2
    window_rows = 2 * shard_rows + 2 * REACH
    subs = subaperture_valid.shape[2]
    n_poke = poke_rows.shape[0]
    each = actuator_codes.size // (n_dir * n_row)
    n_mine = chips * each
    n_local = mirrors * SPAN * NA
    lanes = 2 * shard_rows * subs
    tiles = lanes // 128
    dma = pltpu.SemaphoreType.DMA
    return pl.pallas_call(
        functools.partial(window_kernel, n_dir, n_row),
        out_shape=pltpu.VMEM((each, n_dir, lanes * chips), BF16),
        in_specs=[ANY, ANY, ANY, ANY, VMEM, VMEM, VMEM],
        out_specs=VMEM,
        scratch_shapes=[
            pltpu.VMEM((mirrors, window_rows, slots, columns), BF16),
            pltpu.VMEM((mirrors, window_rows, SPAN * NA, columns), BF16),
            pltpu.VMEM((2, n_local, n_dir * 128), F32),
            pltpu.VMEM((n_local, n_dir * 128), BF16),
            pltpu.VMEM((n_mine * n_dir, 128), F32),
            pltpu.VMEM((tiles, n_mine, n_dir, 128), BF16),
            pltpu.VMEM((n_mine, n_poke), BF16),
            pltpu.VMEM((n_poke, n_local), BF16),
            pltpu.VMEM((n_mine, n_local), BF16),
            pltpu.VMEM((n_mine, 1), I32),
            pltpu.VMEM((1, n_local), I32),
            pltpu.VMEM((2 * n_dir, mirrors, 1, shard_rows), I32),
            pltpu.VMEM((n_dir, mirrors, 1, 2 * subs), I32),
            pltpu.VMEM((2 * n_dir, 1, shard_rows // 2, subs), I32),
            pltpu.SMEM((2 * n_dir, mirrors, 1, shard_rows), I32),
            pltpu.VMEM((n_dir * mirrors, 2 * subs), I32),
            pltpu.VMEM((shard_rows, n_dir, subs), I32),
            pltpu.VMEM((2 * n_dir * mirrors, 1, 256), F32),
            pltpu.VMEM((tiles * n_dir, 1, 128), F32),
            pltpu.VMEM((n_poke // 128, 128, 1), I32),
            dma((15, tiles)), dma((15, tiles)), dma, dma, dma((mirrors,)), dma((mirrors,)), dma, dma,
            dma((n_dir, 2)), dma((n_dir, 2)), dma((n_dir,)), dma((n_dir,)),
            dma((n_dir, 2)), dma((n_dir, 2)), dma((tiles,)), dma((5,)),
        ],
        compiler_params=pltpu.CompilerParams(collective_id=0, has_side_effects=True, vmem_limit_bytes=62_500_000),
        name="window",
    )(
        influence.transpose(0, 1, 3, 2),
        foot_rows.reshape(mirrors, 1, shard_rows),
        foot_columns.reshape(mirrors, 1, 2 * subs),
        subaperture_valid,
        actuator_codes,
        poke_rows.reshape(1, -1),
        poke_rows.reshape(-1, 128),
    )


def solution(mesh):
    return jax.shard_map(
        shards,
        mesh=mesh,
        in_specs=(
            P(None, "row", None, None),
            P("dir", None, "row"),
            P("dir", None, None),
            P(),
            P(),
            P("dir", "row", None),
        ),
        out_specs=P(("dir", "row"), None, None),
        check_vma=False,
    )
```

```python
import functools

import jax
import jax.numpy as jnp
from jax import lax
from jax.experimental import pallas as pl
from jax.experimental.pallas import tpu as pltpu
from jax.sharding import PartitionSpec as P

NAR = 48
NA = 48
REACH = 2
SPAN = 7
MESH = pl.DeviceIdType.MESH
ANY = pl.BlockSpec(memory_space=pl.ANY)
VMEM = pl.BlockSpec(memory_space=pltpu.VMEM)

AROUND = (
    (0, 1), (1, 0), (0, 3), (3, 0), (1, 1), (3, 3), (1, 3), (3, 1),
    (2, 1), (1, 2), (2, 3), (3, 2), (0, 2), (2, 0), (2, 2),
)
PLACE = tuple((3 * w - 6) // 8 + 1 for w in range(12))
REACHED = ((0, 5), (1, 4), (1, 5), (2, 5))
ORDER = [(k, m) for m in (1, 2, 3, 4, 5) for k in range(3)] + [(k, m) for m in (0, 6) for k in range(3)]
SOON = 768
BF16, F32, I32 = jnp.bfloat16, jnp.float32, jnp.int32


def iota(shape, axis):
    return lax.broadcasted_iota(I32, shape, axis)


def over(value, divisor):
    return jnp.right_shift(value * (65536 // divisor + 1), 16)


def sign_of(code_values, row_values):
    odd = jnp.bitwise_and(lax.population_count(jnp.bitwise_and(code_values, row_values)), 1)
    return jnp.where(odd == 0, 1.0, -1.0).astype(jnp.float8_e4m3fn)


def dot(a, b):
    return jnp.dot(a, b, preferred_element_type=F32)


def halves(codes):
    return jnp.right_shift(codes, 7).astype(F32).astype(BF16), jnp.bitwise_and(codes, 127).astype(F32).astype(BF16)


def window_kernel(n_dir, n_row, own, foot_rows, foot_cols, valid, codes_in, pokes_lane_in, pokes_tile_in, out,
                  window, frames, sums, weights, staged, ready, left, right, gram, mine, local,
                  feet_land, cols_land, valid_land, feet, cols_mat, valid_mat, picks, mask,
                  poke_cols, codes, pokes_lane, pokes_tile, far_send, far_recv, halo_send, halo_recv, pair_send, pair_recv, relay_send, relay_recv,
                  feet_send, feet_recv, cols_send, cols_recv, valid_send, valid_recv, keep_sem, own_sem):
    me_dir, me = lax.axis_index("dir"), lax.axis_index("row")
    core = lax.rem(me, 2)
    chip = lax.div(me, 2)
    chips = n_row // 2
    x, y = lax.div(chip, 4), lax.rem(chip, 4)
    rows = own.shape[1]
    mirrors, window_rows, slots, columns = window.shape
    frame = frames.shape[2]
    lanes = out.shape[2] // chips
    each = out.shape[0]
    tiles = lanes // 128

    def chip_at(dx, dy):
        return lax.rem(x + dx, 4) * 4 + lax.rem(y + dy, 4)

    barrier = pltpu.get_barrier_semaphore()

    def greet(there_dir, there):
        pl.semaphore_signal(barrier, inc=1, device_id=(there_dir, there), device_id_type=MESH)

    beside = lax.rem(2 * chip + 3 * core - 1 + n_row, n_row)
    twin = 2 * chip + 1 - core
    greet(me_dir, beside)
    for hop in range(n_dir):
        there = lax.rem(me_dir + hop, n_dir)
        if hop:
            greet(there, me)
        greet(there, twin)
    for dx, dy in AROUND:
        greet(me_dir, chip_at(dx, dy) * 2 + core)

    keeps = [
        pltpu.make_async_copy(own, window.at[:, pl.ds(REACH + rows * core, rows)], own_sem.at[0]),
        pltpu.make_async_copy(foot_rows, feet_land.at[core * n_dir + me_dir], own_sem.at[1]),
        pltpu.make_async_copy(foot_cols, cols_land.at[me_dir], own_sem.at[2]),
        pltpu.make_async_copy(valid, valid_land.at[core * n_dir + me_dir], own_sem.at[3]),
    ]
    tables = [
        pltpu.make_async_copy(codes_in, codes, own_sem.at[5]),
        pltpu.make_async_copy(pokes_tile_in, pokes_tile, own_sem.at[6]),
        pltpu.make_async_copy(pokes_lane_in, pokes_lane, own_sem.at[7]),
    ]
    for copy in keeps + tables:
        copy.start()

    pl.semaphore_wait(barrier, 2 * n_dir + len(AROUND))

    def remote(src, dst, send_sem, recv_sem, target):
        return pltpu.make_async_remote_copy(
            src_ref=src, dst_ref=dst, send_sem=send_sem, recv_sem=recv_sem,
            device_id=target, device_id_type=MESH,
        )

    far_edge = REACH + 2 * rows
    halo = remote(own.at[:, pl.ds((rows - REACH) * core, REACH)],
                  window.at[:, pl.ds(far_edge * (1 - core), REACH)], halo_send, halo_recv, (me_dir, beside))
    halo.start()
    pair = [
        remote(own.at[k], window.at[k, pl.ds(REACH + rows * core, rows)], pair_send.at[k], pair_recv.at[k],
               (me_dir, twin))
        for k in range(mirrors)
    ]
    for copy in pair:
        copy.start()
    small = []
    for hop in range(n_dir):
        there = lax.rem(me_dir + hop, n_dir)
        for side in range(2):
            if hop == 0 and side == 0:
                continue
            target = (there, me if side == 0 else twin)
            small.append(remote(foot_rows, feet_land.at[core * n_dir + me_dir],
                                feet_send.at[hop, side], feet_recv.at[hop, side], target))
            small.append(remote(valid, valid_land.at[core * n_dir + me_dir],
                                valid_send.at[hop, side], valid_recv.at[hop, side], target))
        if hop:
            small.append(remote(foot_cols, cols_land.at[me_dir], cols_send.at[hop], cols_recv.at[hop],
                                (there, me)))
    for copy in small:
        copy.start()

    for copy in tables:
        copy.wait()

    n_mine, n_poke = left.shape
    n_local = right.shape[1]
    table = [halves(codes[k]) for k in range(mirrors)]
    at = iota((n_mine, 1), 0)
    at = at + each * (over(at, each) + core)
    at_row = over(at, NA)
    at_col = at - NA * at_row
    per_dir = mirrors * NAR // n_dir
    upper = jnp.zeros((n_mine, NA), F32)
    lower = jnp.zeros((n_mine, NA), F32)
    for k in range(mirrors):
        hot = (iota((n_mine, NAR), 1) == at_row + (per_dir * me_dir - NAR * k)).astype(F32).astype(BF16)
        upper += dot(hot, table[k][0])
        lower += dot(hot, table[k][1])
    picked = jnp.where(iota((n_mine, NA), 1) == at_col, upper * 128.0 + lower, 0.0)
    mine[...] = jnp.sum(picked, axis=1, keepdims=True).astype(I32)

    lane = iota((1, n_local), 1)
    block = over(lane, NA)
    tile_of = (iota((NA, n_local), 0) == lane - NA * block).astype(F32).astype(BF16)
    row_id = iota((NAR, n_local), 0)
    found = jnp.zeros((1, n_local), F32)
    for k in range(mirrors):
        spread = dot(table[k][0], tile_of) * 128.0 + dot(table[k][1], tile_of)
        third = over(block, mirrors)
        band = jnp.where(third < SPAN - 2, third + 1, (SPAN - 1) * (third - (SPAN - 2)))
        wanted = jnp.where(block - mirrors * third == k, band + 3 * chip - 2, -1)
        found += jnp.sum(jnp.where(row_id == wanted, spread, 0.0), axis=0, keepdims=True)
    local[...] = found.astype(I32)

    turned = jnp.transpose(pokes_tile[...])
    for j in range(n_poke // 128):
        poke_cols[j] = turned[:, j : j + 1]
    def right_of(columns):
        @pl.loop(0, n_poke // 128)
        def _(j):
            part = pl.ds(pl.multiple_of(j * 128, 128), 128)
            right[part, columns] = sign_of(poke_cols[j], local[:, columns])

    right_of(slice(0, SOON))

    relay = remote(window.at[:, pl.ds(far_edge * core, REACH)], window.at[:, pl.ds(far_edge * core, REACH)],
                   relay_send, relay_recv, (me_dir, twin))

    @pl.loop(0, n_mine // 144)
    def _(step):
        part = pl.ds(pl.multiple_of(step * 144, 144), 144)
        left[part, :] = sign_of(mine[part, :], pokes_lane[...])

    gram[:, :SOON] = dot(left[...], right[:, :SOON]).astype(BF16)

    for copy in keeps:
        copy.wait()
    for copy in small:
        copy.wait()
    to_scalar = pltpu.make_async_copy(feet_land, feet, own_sem.at[4])
    to_scalar.start()
    for d in range(n_dir):
        for k in range(mirrors):
            cols_mat[d * mirrors + k : d * mirrors + k + 1, :] = cols_land[d, k]
        for i in range(rows):
            valid_mat[i, d : d + 1, :] = valid_land[i // 2 * n_dir + d, 0, i % 2 : i % 2 + 1, :]
    n_cols = cols_mat.shape[1]
    subs = n_cols // 2
    wide = picks.shape[2]
    def pick(t):
        lane = iota((1, wide), 1) - 32 * t
        inside = (lane >= 0) & (lane < n_cols)
        column = 2 * jnp.where(lane >= subs, lane - subs, lane)
        for first in range(2):
            wanted = jnp.where(inside, column + 1 - first, -1)
            hot = (iota((n_cols, wide), 0) == wanted).astype(F32).astype(BF16)
            value = jnp.where(inside, dot(cols_mat[...].astype(F32).astype(BF16), hot), -1.0)
            for r in range(n_dir * mirrors):
                picks[first * n_dir * mirrors + r] = value[r : r + 1, :]

    lane = iota((1, lanes), 1)
    hot = (iota((subs, lanes), 0) == lane - subs * over(lane, subs)).astype(F32).astype(BF16)
    total = jnp.zeros((n_dir, lanes), F32)
    for i in range(rows):
        value = dot(valid_mat[i].astype(F32).astype(BF16), hot)
        total += jnp.where((lane >= n_cols * i) & (lane < n_cols * (i + 1)), value, 0.0)
    total = total * (0.5 * n_poke ** (-0.5))
    for t in range(tiles):
        for d in range(n_dir):
            mask[t * n_dir + d] = total[d : d + 1, 128 * t : 128 * (t + 1)]

    to_scalar.wait()
    for copy in pair:
        copy.wait()

    def fill(some):
        for w in some:
            start = PLACE[w]
            if 2 <= w <= 4:
                start = start + 1 - lax.div(chip + chips - 1, chips)
            if 8 <= w <= 9:
                start = start - lax.div(chip + 1, chips)
            part = pl.ds(start * NA if isinstance(start, int) else pl.multiple_of(start * NA, NA), slots)
            for k in range(mirrors):
                frames[k, w] = jnp.zeros(frames.shape[2:], BF16)
                frames[k, w, part, :columns] = window[k, w]

    fill(range(REACH, far_edge))

    def far(n, t, order):
        dx, dy = AROUND[n] if order == 0 else AROUND[n][::-1]
        there = chip_at(dx, dy)
        return remote(
            ready.at[t, pl.ds(there * each, each)],
            out.at[:, :, pl.ds(pl.multiple_of(chip * lanes + 128 * t, 128), 128)],
            far_send.at[n, t], far_recv.at[n, t], (me_dir, there * 2 + core),
        )

    def keep(t):
        return pltpu.make_async_copy(
            ready.at[t, pl.ds(chip * each, each)],
            out.at[:, :, pl.ds(pl.multiple_of(chip * lanes + 128 * t, 128), 128)],
            keep_sem.at[t],
        )

    col_id = iota((frames.shape[3], wide), 0).astype(F32).astype(BF16)
    one, zero = jnp.ones((), BF16), jnp.zeros((), BF16)
    lane = iota((1, wide), 1)
    def sample(i):
        low, many = REACHED[i]
        turn = jnp.where(lane < 32 * i + subs, -1.0, 1.0)
        turn, back = turn.astype(BF16), (-turn).astype(BF16)
        pick(i)

        @pl.loop(0, n_dir)
        def _(d):
            block = pl.ds(pl.multiple_of(d * 128, 128), 128)
            for k in range(mirrors):
                later = picks[d * mirrors + k].astype(BF16)
                first = picks[(n_dir + d) * mirrors + k].astype(BF16)
                hot = jnp.where(col_id == later, one, zero) + jnp.where(col_id == first, turn, zero)
                picked = []
                for a in range(2):
                    row = 2 * i + a
                    at = feet[row // rows * n_dir + d, k, 0, row % rows]
                    w = jnp.clip(at - 2 * rows * chip + REACH, 0, window_rows - 1)
                    picked.append(frames[k, w, pl.ds(low * NA, many * NA), :])
                part = dot(jnp.concatenate(picked, axis=1), jnp.concatenate([hot * back, hot], axis=0))
                for n, (k_of, m) in enumerate(ORDER):
                    if k_of != k:
                        continue
                    at = pl.ds(n * NA, NA)
                    if low <= m < low + many:
                        here = part[(m - low) * NA : (m - low + 1) * NA, :128]
                        after = part[(m - low) * NA : (m - low + 1) * NA, 128:]
                    else:
                        here = after = jnp.zeros((NA, 128), F32)
                    if i == 1:
                        sums[0, at, block] = here
                        sums[1, at, block] = after
                    elif i == 0:
                        weights[at, block] = here.astype(BF16)
                        sums[0, at, block] += after
                    else:
                        weights[at, block] = (here + sums[1, at, block]).astype(BF16)
                        sums[1, at, block] = after

    def deliver(t, depth):
        @pl.loop(0, n_dir // 2)
        def _(c):
            part = dot(gram[:, :depth], weights[:depth, pl.ds(pl.multiple_of(c * 256, 256), 256)])
            for e in range(2):
                d = 2 * c + e
                staged[pl.ds(d, n_mine, stride=n_dir), :] = part[:, 128 * e : 128 * (e + 1)] * mask[t * n_dir + d]

        @pl.loop(0, chips)
        def _(b):
            block = staged[pl.ds(pl.multiple_of(b * each * n_dir, n_dir), each * n_dir), :]
            ready[t, pl.ds(b * each, each)] = block.reshape(each, n_dir, 128).astype(BF16)

        for order in range(2):
            @pl.when(core == order)
            def _(order=order):
                for n in range(len(AROUND)):
                    far(n, t, order).start()
        keep(t).start()

    sample(1)
    halo.wait()
    relay.start()
    sample(2)
    deliver(2, SOON)
    relay.wait()
    right_of(slice(SOON, n_local))
    gram[:, SOON:] = dot(left[...], right[:, SOON:]).astype(BF16)
    fill((0, 1, far_edge, far_edge + 1))
    sample(0)
    deliver(0, n_local)
    weights[...] = sums[0].astype(BF16)
    deliver(1, n_local)
    sample(3)
    deliver(3, n_local)
    weights[...] = sums[1].astype(BF16)
    deliver(4, n_local)

    for t in range(tiles):
        keep(t).wait()
        for n in range(len(AROUND)):
            far(n, t, 0).wait()


def shards(influence, foot_rows, foot_columns, actuator_codes, poke_rows, subaperture_valid):
    mirrors, shard_rows, columns, slots = influence.shape
    n_dir, n_row = lax.axis_size("dir"), lax.axis_size("row")
    chips = n_row // 2
    window_rows = 2 * shard_rows + 2 * REACH
    subs = subaperture_valid.shape[2]
    n_poke = poke_rows.shape[0]
    each = actuator_codes.size // (n_dir * n_row)
    n_mine = chips * each
    n_local = mirrors * SPAN * NA
    lanes = 2 * shard_rows * subs
    tiles = lanes // 128
    dma = pltpu.SemaphoreType.DMA
    return pl.pallas_call(
        functools.partial(window_kernel, n_dir, n_row),
        out_shape=pltpu.VMEM((each, n_dir, lanes * chips), BF16),
        in_specs=[ANY] * 7,
        out_specs=VMEM,
        scratch_shapes=[
            pltpu.VMEM((mirrors, window_rows, slots, columns), BF16),
            pltpu.VMEM((mirrors, window_rows, SPAN * NA, 256), BF16),
            pltpu.VMEM((2, n_local, n_dir * 128), F32),
            pltpu.VMEM((n_local, n_dir * 128), BF16),
            pltpu.VMEM((n_mine * n_dir, 128), F32),
            pltpu.VMEM((tiles, n_mine, n_dir, 128), BF16),
            pltpu.VMEM((n_mine, n_poke), jnp.float8_e4m3fn),
            pltpu.VMEM((n_poke, n_local), jnp.float8_e4m3fn),
            pltpu.VMEM((n_mine, n_local), BF16),
            pltpu.VMEM((n_mine, 1), I32),
            pltpu.VMEM((1, n_local), I32),
            pltpu.VMEM((2 * n_dir, mirrors, 1, shard_rows), I32),
            pltpu.VMEM((n_dir, mirrors, 1, 2 * subs), I32),
            pltpu.VMEM((2 * n_dir, 1, shard_rows // 2, subs), I32),
            pltpu.SMEM((2 * n_dir, mirrors, 1, shard_rows), I32),
            pltpu.VMEM((n_dir * mirrors, 2 * subs), I32),
            pltpu.VMEM((shard_rows, n_dir, subs), I32),
            pltpu.VMEM((2 * n_dir * mirrors, 1, 256), F32),
            pltpu.VMEM((tiles * n_dir, 1, 128), F32),
            pltpu.VMEM((n_poke // 128, 128, 1), I32),
            pltpu.VMEM(actuator_codes.shape, I32),
            pltpu.VMEM((1, n_poke), I32),
            pltpu.VMEM((n_poke // 128, 128), I32),
            dma((15, tiles)), dma((15, tiles)), dma, dma, dma((mirrors,)), dma((mirrors,)), dma, dma,
            dma((n_dir, 2)), dma((n_dir, 2)), dma((n_dir,)), dma((n_dir,)),
            dma((n_dir, 2)), dma((n_dir, 2)), dma((tiles,)), dma((8,)),
        ],
        compiler_params=pltpu.CompilerParams(collective_id=0, has_side_effects=True, vmem_limit_bytes=62_500_000),
        name="window",
    )(
        influence.transpose(0, 1, 3, 2),
        foot_rows.reshape(mirrors, 1, shard_rows),
        foot_columns.reshape(mirrors, 1, 2 * subs),
        subaperture_valid,
        actuator_codes,
        poke_rows.reshape(1, -1),
        poke_rows.reshape(-1, 128),
    )


def solution(mesh):
    return jax.shard_map(
        shards,
        mesh=mesh,
        in_specs=(
            P(None, "row", None, None),
            P("dir", None, "row"),
            P("dir", None, None),
            P(),
            P(),
            P("dir", "row", None),
        ),
        out_specs=P(("dir", "row"), None, None),
        check_vma=False,
    )
```
